32 devices in a mesh: row: 8 (over z, x), col: 2 (over y), tm: 2 (over core).
Axes of the slice: x: 2, y: 2, z: 4, core: 2. Of those that a mesh axis runs over, the one named last changes fastest.
Arguments:
- queries: bfloat16 [4096, 6144], P(('row', 'tm'), 'col'), may hold values from -6 to 6
- k_cache: bfloat16 [8, 2048, 6144], P('row', 'tm', 'col'), may hold values from -6 to 6
- v_cache: bfloat16 [8, 2048, 6144], P('row', 'tm', 'col'), may hold values from -48 to 48
- lists: int32 [8, 4, 4], P('row'), may hold values from 0 to 15, all different within a row
- counts: int32 [8, 4], P('row'), may hold values from 1 to 4
- w_out: bfloat16 [6144, 6144], P('row', 'col'), may hold values from -0.078125 to 0.078125
Outputs:
- projected: bfloat16 [4096, 6144], P(('row', 'tm'), 'col')
The draws below stay inside these ranges and needn't reach their ends.
Inputs may be any that keep to these rules, and one draw needn't show every extreme that they name: `lists`: the 4 entries of one list name different cached blocks of the stream.
All inputs are finite; a program needn't handle non-finite values.
Results may differ from the reference program's by a relative error of at most 0.0057.
Values may be sent and summed in bfloat16 or wider, within the bound.
No kernel may reach another device: no remote copies, remote signals or barrier semaphores. Data moves between devices by JAX's collectives and lax.ppermute only.
A program may use at most 128 MiB of HBM per device.

```python
import math
import jax
import jax.numpy as jnp
from jax import lax

HEADS = 48
HD = 128
D = 6144
BLK = 128
LIST = 4
QTOK = 256
CB = 8
QB = 2
STREAMS = 8
TOKENS = 4096
N_TM = 2


def set_ends(drawn, stream_key, least, top_value):
    extent = drawn.shape
    spot = [jax.random.randint(jax.random.fold_in(stream_key, axis), (), 0, extent[axis]) for axis in range(len(extent))]
    drawn = drawn.at[tuple(spot)].set(least)
    longest = extent.index(max(extent))
    spot[longest] = (spot[longest] + 1) % extent[longest]
    return drawn.at[tuple(spot)].set(top_value)


def levels(own_key, dims, split, low, high):
    def one(dim, parts):
        heights = jax.random.uniform(jax.random.fold_in(jax.random.fold_in(own_key, 6), dim), (parts,), jnp.float32, low / len(split), high / len(split))
        return jnp.repeat(jnp.exp(heights), dims[dim] // parts).reshape((-1,) + (1,) * (len(dims) - dim - 1))

    factor_of = one(*split[0])
    for cut in split[1:]:
        factor_of = factor_of * one(*cut)
    return factor_of


def distinct(rng, rows, amount, top, lift):
    ranking = jax.random.permutation(jax.random.fold_in(rng, 1), amount)
    favour = ranking
    for power in range(3):
        favour = favour * favour // amount
    favour = favour * lift // amount
    lots = jax.random.randint(jax.random.fold_in(rng, 2), (rows, amount), 0, 4096) + favour
    sure = jax.random.permutation(jax.random.fold_in(rng, 3), rows)[jnp.arange(amount) % rows]
    lots = jnp.where(jnp.arange(rows)[:, None] == sure[None, :], 1 << 14, lots)
    score = lots * amount + jnp.arange(amount)
    return lax.top_k(score.astype(jnp.int32), top)[1].astype(jnp.int32)


def scatter_about(key, extent, deviation, bound, shards=(), kind=jnp.bfloat16):
    values = jax.random.normal(key, extent, jnp.float32) * deviation
    if len(shards) > 0:
        values = levels(key, extent, shards, -0.22, 0.18) * values
    return jnp.clip(values, min=-bound, max=bound).astype(kind)


def setup_inputs(seed: int = 0) -> dict:
    key_list = jax.random.split(jax.random.key(seed), 7)
    return {
        "queries": scatter_about(key_list[0], (TOKENS, D), 1.0, 6.0, ((0, 16), (1, 2))),
        "k_cache": scatter_about(key_list[1], (STREAMS, N_TM * CB * BLK, D), 1.0, 6.0, ((0, 8), (1, 2), (2, 2))),
        "v_cache": scatter_about(key_list[2], (STREAMS, N_TM * CB * BLK, D), 8.0, 48.0, ((0, 8), (1, 2), (2, 2))),
        "lists": distinct(key_list[3], STREAMS * (N_TM * QB), N_TM * CB, LIST, 2048).reshape((STREAMS, N_TM * QB, LIST)),
        "counts": set_ends(jax.random.randint(key_list[4], (STREAMS, N_TM * QB), 1, LIST + 1), jax.random.fold_in(key_list[4], 1), 1, LIST).astype(jnp.int32),
        "w_out": scatter_about(key_list[5], (D, D), D ** -0.5, 0.078125, ((0, 8), (1, 2))),
    }


def stream_attention(packed):
    stream_queries, stream_keys, stream_values, stream_lists, stream_counts = packed
    query_count = stream_lists.shape[0]
    shaped = stream_queries.reshape(query_count, BLK, HEADS, HD).astype(jnp.float32)
    key_blocks = stream_keys.reshape(-1, BLK, HEADS, HD)
    value_blocks = stream_values.reshape(-1, BLK, HEADS, HD)
    key_taken = key_blocks[stream_lists].astype(jnp.float32)
    value_taken = value_blocks[stream_lists].astype(jnp.float32)
    scores = jnp.einsum('bqhd,bjkhd->bhqjk', shaped, key_taken) * (1.0 / math.sqrt(HD))
    weights = jax.nn.sigmoid(scores - math.log(LIST * BLK))
    entry_live = jnp.arange(LIST)[None, :] < stream_counts[:, None]
    weights = jnp.where(entry_live[:, None, None, :, None], weights, 0.0).astype(jnp.bfloat16)
    mixed = jnp.einsum('bhqjk,bjkhd->bqhd', weights.astype(jnp.float32), value_taken)
    return mixed.astype(jnp.bfloat16).reshape(query_count * BLK, HEADS * HD)

def reference(queries, k_cache, v_cache, lists, counts, w_out):
    grouped = queries.reshape(STREAMS, N_TM * QTOK, D)
    heads_out = lax.map(stream_attention, (grouped, k_cache, v_cache, lists, counts))
    heads_out = heads_out.reshape(TOKENS, D)
    return jnp.dot(heads_out, w_out, preferred_element_type=jnp.float32).astype(jnp.bfloat16)
```

```python
import functools
import math

import jax
import jax.numpy as jnp
from jax import lax
from jax.experimental import pallas as pl
from jax.experimental.pallas import tpu as pltpu
from jax.sharding import PartitionSpec as P


HD = 128
BLK = 128
LIST = 4
PAIR = 2


def swapped(value, axis, mask):
    pairs = [(source, source ^ mask) for source in range(lax.axis_size(axis))]
    return lax.ppermute(value, axis, pairs)


def crossed(value, row_mask):
    count = lax.axis_size("row")
    pairs = [(2 * r + t, 2 * (r ^ row_mask) + 1 - t) for r in range(count) for t in range(2)]
    return lax.ppermute(value, ("row", "tm"), pairs)


def upper(row):
    return (row // PAIR) % 2


def handed(value):
    count = lax.axis_size("row")
    pairs = [
        (2 * r + 1 - upper(r), 2 * (r ^ PAIR) + 1 - upper(r ^ PAIR)) for r in range(count)
    ]
    return lax.ppermute(value, ("row", "tm"), pairs)


def attention_kernel(
    head_count, span, first, lists, counts, core, q_own, q_peer, k_own, v_own, k_peer, v_peer,
    out, k_buf, v_buf, k_sem, v_sem
):
    step = pl.program_id(0)
    block = first + step
    half = head_count * HD
    me = core[0]

    def copies(b, slot, j, mine):
        entry = lists[b * LIST + j]
        rows = pl.ds(pl.multiple_of(lax.rem(entry, span) * BLK, BLK), BLK)
        columns = pl.ds(pl.multiple_of(me * half, HD), half)
        place = pl.ds(j * BLK, BLK)
        k_from = k_own.at[rows, columns] if mine else k_peer.at[rows, :]
        v_from = v_own.at[rows, columns] if mine else v_peer.at[rows, :]
        return (
            pltpu.make_async_copy(k_from, k_buf.at[slot, place, :], k_sem.at[slot, j]),
            pltpu.make_async_copy(v_from, v_buf.at[slot, place, :], v_sem.at[slot, j]),
        )

    def fetch(b, slot):
        for j in range(LIST):
            mine = lax.div(lists[b * LIST + j], span) == me

            @pl.when(mine)
            def _():
                for copy in copies(b, slot, j, True):
                    copy.start()

            @pl.when(jnp.logical_not(mine))
            def _():
                for copy in copies(b, slot, j, False):
                    copy.start()

    slot = lax.rem(step, 2)

    @pl.when(step == 0)
    def _():
        fetch(block, slot)

    @pl.when(step + 1 < pl.num_programs(0))
    def _():
        fetch(block + 1, 1 - slot)

    for j in range(LIST):
        for copy in copies(block, slot, j, False):
            copy.wait()

    own = lax.div(first, pl.num_programs(0)) == me
    live = lax.broadcasted_iota(jnp.int32, (1, LIST * BLK), 1) < counts[block] * BLK
    scale = math.log2(math.e) / math.sqrt(HD)
    for head in range(head_count):
        part = slice(head * HD, (head + 1) * HD)
        query = jnp.where(own, q_own[:, part], q_peer[:, part])
        scores = lax.dot_general(
            query, k_buf[slot, :, part], (((1,), (1,)), ((), ())),
            preferred_element_type=jnp.float32,
        )
        power = jnp.minimum(math.log2(LIST * BLK) - scores * scale, 126.0)
        weights = 1.0 / (1.0 + jnp.exp2(power))
        weights = jnp.where(live, weights, 0.0).astype(jnp.bfloat16)
        mixed = jnp.dot(weights, v_buf[slot, :, part], preferred_element_type=jnp.float32)
        out[:, part] = mixed.astype(jnp.bfloat16)


def attend(span_index, lists, counts, core, queries, peer_queries, keys, values, peer_keys, peer_values):
    half = peer_queries.shape[1]
    blocks = queries.shape[0] // BLK
    span = keys.shape[0] // BLK

    def own_map(b, lists, counts, core):
        return (b, core[0])

    def peer_map(b, lists, counts, core):
        return (b, 0)

    anywhere = pl.BlockSpec(memory_space=pl.ANY)
    return pl.pallas_call(
        functools.partial(attention_kernel, half // HD, span, span_index * blocks),
        out_shape=jax.ShapeDtypeStruct((blocks * BLK, half), jnp.bfloat16),
        grid_spec=pltpu.PrefetchScalarGridSpec(
            num_scalar_prefetch=3,
            grid=(blocks,),
            in_specs=[
                pl.BlockSpec((BLK, half), own_map),
                pl.BlockSpec((BLK, half), peer_map),
                anywhere, anywhere, anywhere, anywhere,
            ],
            out_specs=pl.BlockSpec((BLK, half), lambda b, *_: (b, 0)),
            scratch_shapes=[
                pltpu.VMEM((2, LIST * BLK, half), jnp.bfloat16),
                pltpu.VMEM((2, LIST * BLK, half), jnp.bfloat16),
                pltpu.SemaphoreType.DMA((2, LIST)),
                pltpu.SemaphoreType.DMA((2, LIST)),
            ],
        ),
        cost_estimate=pl.CostEstimate(
            flops=4 * blocks * BLK * LIST * BLK * half,
            bytes_accessed=4 * blocks * LIST * BLK * half,
            transcendentals=blocks * BLK * LIST * BLK * half // HD,
        ),
        name="attention",
    )(lists, counts, core, queries, peer_queries, keys, values, peer_keys, peer_values)


def product_kernel(table, *refs):
    count = len(refs) - 13
    rows, weights, outs = refs[:4], refs[4 : 4 + count], refs[4 + count : 8 + count]
    a_buf, w_buf, total, a_sem, w_sem = refs[8 + count :]
    tile = outs[0].shape[0]
    depth = w_buf.shape[1]

    def copies(i):
        columns = pl.ds(pl.multiple_of(table[4 + i] * depth, HD), depth)
        taken = [
            pltpu.make_async_copy(
                row.at[:, columns], a_buf.at[i, pl.ds(s * tile, tile), :], a_sem.at[i, s]
            )
            for s, row in enumerate(rows)
        ]
        return [pltpu.make_async_copy(weights[i], w_buf.at[i], w_sem.at[i])] + taken

    for i in range(count):
        for copy in copies(i):
            copy.start()
    for i in range(count):
        for copy in copies(i):
            copy.wait()
        term = jnp.dot(a_buf[i], w_buf[i], preferred_element_type=jnp.float32)
        total[...] = term if i == 0 else total[...] + term
    for k, out in enumerate(outs):
        place = (table[k // 2] * 2 + lax.rem(table[2] + k + k // 2, 2)) * tile
        out[...] = total[pl.ds(pl.multiple_of(place, tile), tile), :].astype(jnp.bfloat16)


def products(table, rows, weights):
    count = len(weights)
    depth, width = weights[0].shape
    tile = rows[0].shape[0]
    anywhere = pl.BlockSpec(memory_space=pl.ANY)
    return pl.pallas_call(
        product_kernel,
        out_shape=[jax.ShapeDtypeStruct((tile, width), jnp.bfloat16)] * 4,
        grid_spec=pltpu.PrefetchScalarGridSpec(
            num_scalar_prefetch=1,
            grid=(1,),
            in_specs=[anywhere] * (4 + count),
            out_specs=[pl.BlockSpec((tile, width), lambda i, table: (0, 0))] * 4,
            scratch_shapes=[
                pltpu.VMEM((count, 4 * tile, depth), jnp.bfloat16),
                pltpu.VMEM((count, depth, width), jnp.bfloat16),
                pltpu.VMEM((4 * tile, width), jnp.float32),
                pltpu.SemaphoreType.DMA((count, 4)),
                pltpu.SemaphoreType.DMA((count,)),
            ],
        ),
        cost_estimate=pl.CostEstimate(
            flops=8 * tile * count * depth * width,
            bytes_accessed=2 * (4 * tile * (count * depth + width) + count * depth * width),
            transcendentals=0,
        ),
        name="products",
    )(table, *rows, *weights)


def plain_products(table, rows, weights):
    depth, width = weights[0].shape
    joined = jnp.zeros((depth * len(weights), width), weights[0].dtype)
    for i, weight in enumerate(weights):
        joined = lax.dynamic_update_slice_in_dim(joined, weight, table[4 + i] * depth, 0)
    stacked = jnp.stack(rows)
    outs = []
    for k in range(4):
        place = table[k // 2] * 2 + (table[2] + k + k // 2) % 2
        taken = lax.dynamic_index_in_dim(stacked, place, 0, keepdims=False)
        product = jnp.dot(taken, joined, preferred_element_type=jnp.float32)
        outs.append(product.astype(jnp.bfloat16))
    return outs


def chunks_of(half):
    sizes = []
    left = half
    while left > 0:
        size = 512 if left >= 1024 else min(256, left)
        sizes.append(size)
        left -= size
    return sizes


def local(queries, k_cache, v_cache, lists, counts, w_out):
    core = lax.axis_index("tm")
    row = lax.axis_index("row")
    col = lax.axis_index("col")
    row_count = lax.axis_size("row")
    col_count = lax.axis_size("col")
    width = queries.shape[1]
    half = width // 2
    depth = w_out.shape[0]
    assert row_count == 4 * col_count and half == 2 * depth
    mine = upper(row)

    masks = [1 << bit for bit in range(row_count.bit_length() - 1) if 1 << bit != PAIR][::-1]
    weights, sizes = [], chunks_of(half)
    for j, size in enumerate(sizes):
        start = core * half + sum(sizes[:j])
        blocks = [lax.dynamic_slice_in_dim(w_out, start, size, 1)]
        for mask in masks:
            moved = []
            for block in blocks:
                moved.append(swapped(block, "row", mask))
            blocks = blocks + moved
        weights.append(blocks)
    origins = [0]
    for mask in masks:
        origins = origins + [origin ^ mask for origin in origins]

    def sent(value):
        taken = lax.dynamic_slice_in_dim(value, (1 - core) * half, half, 1)
        return swapped(taken, "tm", 1)

    keys, values = k_cache[0], v_cache[0]
    peer_queries, peer_keys = sent(queries), sent(keys)
    peer_values = sent(values)
    holds_own = core == mine
    rows_here, rows_there = [], []
    for part in range(2):
        heads_out = attend(
            part, lists.reshape(-1), counts.reshape(-1), core.reshape(1), queries,
            peer_queries, keys, values, peer_keys, peer_values,
        )
        arrived = handed(heads_out)
        block = jnp.where(holds_own, heads_out, arrived)
        bit = 1
        while bit < col_count:
            other = swapped(block, "col", bit)
            low = (col // bit) % 2 == 0
            block = jnp.concatenate(
                [jnp.where(low, block, other), jnp.where(low, other, block)], 1
            )
            bit *= 2
        rows_here.append(block)
        rows_there.append(swapped(block, "tm", 1))

    places = [((row ^ o) // 4) * 2 + (row ^ o) % 2 for o in origins]
    pair_source = jnp.where(holds_own, 1, 0)
    table = jnp.stack([pair_source, 1 - pair_source, core, core] + places).astype(jnp.int32)
    multiply = products if depth % HD == 0 else plain_products

    near, far = [], []
    for blocks in weights:
        pair_same, pair_cross, own_cross, own_same = multiply(table, rows_here + rows_there, blocks)
        from_same = swapped(pair_same, "row", PAIR)
        from_cross = crossed(pair_cross, PAIR)
        from_core = swapped(own_cross, "tm", 1)
        near.append(own_same.astype(jnp.float32) + from_same.astype(jnp.float32))
        far.append(from_core.astype(jnp.float32) + from_cross.astype(jnp.float32))
    near = jnp.concatenate(near, 1)
    far = jnp.concatenate(far, 1)
    result = jnp.concatenate(
        [jnp.where(core == 0, near, far), jnp.where(core == 0, far, near)], 1
    )
    return result.astype(jnp.bfloat16)


def solution(mesh):
    placed = (
        P(("row", "tm"), "col"),
        P("row", "tm", "col"),
        P("row", "tm", "col"),
        P("row", None, None),
        P("row", None),
        P("row", "col"),
    )
    return jax.shard_map(
        local, mesh=mesh, in_specs=placed, out_specs=P(("row", "tm"), "col"), check_vma=False
    )
```
